32 devices in a mesh: groups: 2 (over x), seq: 16 (over z, y, core).
Axes of the slice: x: 2, y: 2, z: 4, core: 2. Of those that a mesh axis runs over, the one named last changes fastest.
Arguments:
- sequence: bfloat16 [8192, 1536], P(('groups', 'seq')), parts along dimension 0, may hold values from -6 to 6
- gain_conv: float32 [1536], replicated, may hold values from 0.25 to 1.75
- conv_weight: float32 [5, 1536], replicated, may hold values from -3 to 3
- gain_attn: float32 [1536], replicated, may hold values from 0.25 to 1.75
- w_query: bfloat16 [1536, 1024], replicated
- w_key: bfloat16 [1536, 128], replicated
- w_value: bfloat16 [1536, 192], replicated, may hold values from -0.15625 to 0.15625
- w_out: bfloat16 [1536, 1536], replicated, may hold values from -0.15625 to 0.15625
- w_left: bfloat16 [1536, 128], replicated, may hold values from -0.15625 to 0.15625
- w_right: bfloat16 [1536, 128], replicated, may hold values from -0.15625 to 0.15625
- w_pair: bfloat16 [3, 3, 128, 128], replicated, may hold values from -0.1875 to 0.1875
Outputs:
- track: bfloat16 [8192, 1536], P(('groups', 'seq')), parts along dimension 0
- pair_map: bfloat16 [512, 256, 128], P(('groups', 'seq')), parts along dimension 0
The draws below stay inside these ranges and needn't reach their ends.
There are 2 independent parts, one for each index of `groups`. The reference program is written for one: setup_inputs(seed, part) draws one part's arguments, and reference() takes and returns one part's arrays. A program takes and returns all parts, laid end to end along the dimension named above; an argument that names none is the same for every part. Nothing has to cross between parts.
All inputs are finite; a program needn't handle non-finite values.
Results may differ from the reference program's by a relative error of at most 0.019.
Values may be sent and summed in bfloat16 or wider, within the bound.
A program may use at most 128 MiB of HBM per device.

```python
import jax
import jax.numpy as jnp
from jax import lax

D = 1536
HEADS = 8
KEY = 128
VAL = 192
PAIR = 128
POOL = 16
CONV = 5
SEQ = 4096
PROWS = 256


def shared_keys(key):
    return jax.random.normal(jax.random.fold_in(key, 11), (D, KEY), jnp.float32) * D ** (-0.5)


def draw_w_key(key, part):
    return shared_keys(key).astype(jnp.bfloat16)


def turned_keys(key):
    base = shared_keys(key)
    flips = jax.random.bernoulli(jax.random.fold_in(key, 31), 0.5, (HEADS, KEY)).astype(jnp.float32) * 2.0 - 1.0
    turned = [jnp.roll(base, 1 + head, axis=1) * flips[head][None, :] for head in range(HEADS)]
    return jnp.stack(turned, axis=1)


def draw_w_query(key, part):
    own = jax.random.normal(jax.random.fold_in(key, 23), (D, HEADS, KEY), jnp.float32) * D ** (-0.5)
    strength = jax.random.uniform(jax.random.fold_in(key, 37), (HEADS,), jnp.float32, 1.5, 2.6)
    coupled = strength[None, :, None] * turned_keys(key) + 0.3 * own
    return coupled.reshape(D, HEADS * KEY).astype(jnp.bfloat16)


def steps_of(key, shape, pieces, low, largest):
    def one(dim, blocks):
        steps = jax.random.uniform(jax.random.fold_in(jax.random.fold_in(key, 6), dim), (blocks,), jnp.float32, low / len(pieces), largest / len(pieces))
        return jnp.repeat(jnp.exp(steps), shape[dim] // blocks).reshape((-1,) + (1,) * (len(shape) - dim - 1))

    level = one(*pieces[0])
    for cut in pieces[1:]:
        level = level * one(*cut)
    return level


def gaussian(rng, shape, scale, reach, cuts=(), kind=jnp.bfloat16):
    level = steps_of(rng, shape, cuts, -0.22, 0.18) if cuts else 1.0
    values = jax.random.normal(rng, shape, jnp.float32) * scale * level
    return jnp.minimum(jnp.maximum(values, -reach), reach).astype(kind)


def setup_inputs(seed: int = 0, part: int = 0) -> dict:
    key_of = jax.random.split(jax.random.key(seed), 12)
    own_keys = jax.random.split(jax.random.fold_in(key_of[11], part), 12)
    return {
        "sequence": gaussian(own_keys[0], (SEQ, D), 1.0, 6.0, ((0, 16),)),
        "gain_conv": jnp.clip(1.0 + 0.15 * jax.random.normal(key_of[1], (D,), jnp.float32), 0.25, 1.75),
        "conv_weight": gaussian(key_of[2], (CONV, D), 0.5, 3.0, (), jnp.float32),
        "gain_attn": jnp.clip(1.0 + 0.15 * jax.random.normal(key_of[3], (D,), jnp.float32), 0.25, 1.75),
        "w_query": draw_w_query(jax.random.fold_in(key_of[11], 71), part),
        "w_key": draw_w_key(jax.random.fold_in(key_of[11], 71), part),
        "w_value": gaussian(key_of[6], (D, VAL), D ** -0.5, 0.15625),
        "w_out": gaussian(key_of[7], (HEADS * VAL, D), (HEADS * VAL) ** -0.5, 0.15625),
        "w_left": gaussian(key_of[8], (D, PAIR), D ** -0.5, 0.15625),
        "w_right": gaussian(key_of[9], (D, PAIR), D ** -0.5, 0.15625),
        "w_pair": gaussian(key_of[10], (3, 3, PAIR, PAIR), (9 * PAIR) ** -0.5, 0.1875),
    }


def rms_norm(values, gain):
    values = values.astype(jnp.float32)
    scale = lax.rsqrt(lax.optimization_barrier(jnp.mean(values * values, axis=-1, keepdims=True)) + 1e-06)
    return values * scale * gain

def reference(sequence, gain_conv, conv_weight, gain_attn, w_query, w_key, w_value, w_out, w_left, w_right, w_pair):
    normed = rms_norm(sequence, gain_conv).astype(jnp.bfloat16)
    padded = jnp.pad(normed.astype(jnp.float32), ((2, 2), (0, 0)))
    convolved = jnp.zeros((SEQ, D), jnp.float32)
    for offset in range(CONV):
        convolved = convolved + conv_weight[offset][None, :] * padded[offset:offset + SEQ]
    first = (sequence.astype(jnp.float32) + convolved).astype(jnp.bfloat16)
    attn_in = rms_norm(first, gain_attn).astype(jnp.bfloat16)
    queries = jnp.dot(attn_in, w_query, preferred_element_type=jnp.float32).astype(jnp.bfloat16)
    keys = jnp.dot(attn_in, w_key, preferred_element_type=jnp.float32).astype(jnp.bfloat16).astype(jnp.float32)
    values = jnp.dot(attn_in, w_value, preferred_element_type=jnp.float32).astype(jnp.bfloat16).astype(jnp.float32)
    block = min(512, SEQ)
    query_blocks = queries.reshape(SEQ // block, block, HEADS, KEY)
    scale = 1.0 / jnp.sqrt(jnp.float32(KEY))

    def attend(query_block):
        scores = jnp.einsum('qhd,kd->hqk', query_block.astype(jnp.float32), keys) * scale
        top = lax.optimization_barrier(jnp.max(scores, axis=-1, keepdims=True))
        expo = jnp.exp(scores - top)
        total = lax.optimization_barrier(jnp.sum(expo, axis=-1))
        rounded = expo.astype(jnp.bfloat16).astype(jnp.float32)
        numer = jnp.einsum('hqk,kv->hqv', rounded, values)
        result = numer / total[..., None]
        return jnp.transpose(result, (1, 0, 2)).reshape(block, HEADS * VAL).astype(jnp.bfloat16)
    attended = lax.map(attend, query_blocks).reshape(SEQ, HEADS * VAL)
    track = (first.astype(jnp.float32) + jnp.dot(attended, w_out, preferred_element_type=jnp.float32)).astype(jnp.bfloat16)
    pooled = lax.optimization_barrier(jnp.mean(track.astype(jnp.float32).reshape(PROWS, POOL, D), axis=1)).astype(jnp.bfloat16)
    left = jnp.dot(pooled, w_left, preferred_element_type=jnp.float32).astype(jnp.bfloat16)
    right = jnp.dot(pooled, w_right, preferred_element_type=jnp.float32).astype(jnp.bfloat16)
    pair0 = (left.astype(jnp.float32)[:, None, :] * right.astype(jnp.float32)[None, :, :]).astype(jnp.bfloat16)
    activated = jax.nn.gelu(pair0.astype(jnp.float32)).astype(jnp.bfloat16)
    grid = jnp.pad(activated, ((1, 1), (1, 1), (0, 0)))
    summed = jnp.zeros((PROWS * PROWS, PAIR), jnp.float32)
    for row_off in range(3):
        for col_off in range(3):
            window = grid[row_off:row_off + PROWS, col_off:col_off + PROWS].reshape(PROWS * PROWS, PAIR)
            summed = summed + jnp.dot(window, w_pair[row_off, col_off], preferred_element_type=jnp.float32)
    pair_map = (pair0.astype(jnp.float32) + summed.reshape(PROWS, PROWS, PAIR)).astype(jnp.bfloat16)
    return (track, pair_map)
```

```python
import functools
import math

import jax
import jax.numpy as jnp
from jax import lax
from jax.experimental import pallas as pl
from jax.experimental.pallas import tpu as pltpu
from jax.sharding import PartitionSpec as P

HEADS = 8
POOL = 16
HALO = 16
PARTS = 2
F32 = jnp.float32
BF16 = jnp.bfloat16


def dot(a, b):
    return jnp.dot(a, b, preferred_element_type=F32)


def dot_t(a, b):
    return lax.dot_general(a, b, (((1,), (1,)), ((), ())), preferred_element_type=F32)


def rms_norm(values, gain):
    scale = lax.rsqrt(jnp.mean(values * values, axis=-1, keepdims=True) + 1e-06)
    return values * scale * gain


def kernel(
    n,
    seq_ref, conv_ref,
    gconv_hbm, gattn_hbm, wq_hbm, wk_hbm, wv_hbm, wo_hbm, wl_hbm, wr_hbm,
    track_hbm, left_ext, right_land,
    gains, wq, wk, wv, wo, wl, wr, track_ref,
    halo, padded, first, attn, q_ref, kv, acc, top, attended,
    own_left, left_halo, turned, stage,
    w_sem, track_sem, halo_send, halo_recv, r_send, l_send, p_send, kv_recv,
    left_send, left_recv, right_send, right_recv,
):
    rows, width = seq_ref.shape
    key = wk.shape[1]
    val = wv.shape[0]
    taps = conv_ref.shape[0]
    reach = taps // 2
    part = rows // PARTS
    chips = n // 2
    half = (chips + 1) // 2
    me = lax.axis_index("seq")
    chip = me // 2
    core = me % 2
    partner = chip * 2 + (1 - core)
    pos = jnp.where(chip % 2 == 0, chip // 2, chips - 1 - chip // 2)

    def chip_at(place):
        place = lax.rem(place + 2 * chips, chips)
        return jnp.where(place < half, 2 * place, 2 * (chips - 1 - place) + 1)

    def mine_at(place):
        return chip_at(place) * 2 + core

    def other_at(place):
        return chip_at(place) * 2 + (1 - core)

    barrier = pltpu.get_barrier_semaphore()

    @pl.loop(1, n)
    def _(step):
        pl.semaphore_signal(barrier, inc=1, device_id={"seq": lax.rem(me + step, n)})

    pairs = (
        (wk_hbm, wk), (wv_hbm, wv), (wq_hbm, wq), (wo_hbm, wo), (wl_hbm, wl), (wr_hbm, wr),
        (gconv_hbm, gains.at[0]), (gattn_hbm, gains.at[1]),
    )
    loads = [pltpu.make_async_copy(s, d, w_sem.at[i]) for i, (s, d) in enumerate(pairs)]
    for load in loads[6:] + loads[:6]:
        load.start()

    def send(src, dst, ssem, rsem, to):
        return pltpu.make_async_remote_copy(
            src_ref=src, dst_ref=dst, send_sem=ssem, recv_sem=rsem, device_id={"seq": to}
        )

    has_prev = me > 0
    has_next = me < n - 1
    prev = lax.rem(me + n - 1, n)
    after = lax.rem(me + 1, n)
    to_next = send(seq_ref.at[pl.ds(rows - HALO, HALO)], halo.at[0], halo_send.at[0], halo_recv.at[0], after)
    to_prev = send(seq_ref.at[pl.ds(0, HALO)], halo.at[1], halo_send.at[1], halo_recv.at[1], prev)

    loads[6].wait()
    loads[7].wait()
    gconv = gains[0:1, :]
    strip = 32
    for start in range(0, rows, strip):
        values = seq_ref[start:start + strip, :].astype(F32)
        padded[HALO + start:HALO + start + strip, :] = rms_norm(values, gconv).astype(BF16).astype(F32)

    pl.semaphore_wait(barrier, n - 1)

    @pl.when(has_next)
    def _():
        to_next.start()

    @pl.when(has_prev)
    def _():
        to_prev.start()

    gattn = gains[1:2, :]

    def mix(start):
        total = seq_ref[start:start + strip, :].astype(F32)
        conv = jnp.zeros((strip, width), F32)
        for tap in range(taps):
            base = HALO + start + tap - reach
            conv = conv + conv_ref[tap:tap + 1, :] * padded[base:base + strip, :]
        one = (total + conv).astype(BF16)
        first[start:start + strip, :] = one
        attn[start:start + strip, :] = rms_norm(one.astype(F32), gattn).astype(BF16)

    right_steps = (chips - 1) // 2
    opposite = chips % 2 == 0
    to_right = mine_at(pos + 1)
    to_left = mine_at(pos - 1)
    by_right = PARTS // 2

    def piece(slot, c):
        return kv.at[slot, c]

    def copy_right(t, c):
        slot = mine_at(pos - t)
        return send(piece(slot, c), piece(slot, c), r_send.at[t, c], kv_recv.at[slot, c], to_right)

    def copy_left(t, c):
        slot = mine_at(pos + t)
        return send(piece(slot, c), piece(slot, c), l_send.at[t, c], kv_recv.at[slot, c], to_left)

    def copy_partner(slot, count, c):
        return send(piece(slot, c), piece(slot, c), p_send.at[count, c], kv_recv.at[slot, c], partner)

    def arrived(slot, c):
        send(piece(slot, c), piece(slot, c), p_send.at[0, c], kv_recv.at[slot, c], partner).wait_recv()

    sent = []

    def go(copy):
        copy.start()
        sent.append(copy)

    def pass_right(t, c):
        if t < right_steps or (opposite and t == right_steps and c < by_right):
            go(copy_right(t, c))

    def pass_left(t, c):
        if t < right_steps or (opposite and t == right_steps and c >= by_right):
            go(copy_left(t, c))

    tail = val - 128
    fold = part // (128 // tail)

    def project(rows_in, c):
        kv[me, c, 0:key, :] = dot(rows_in, wk[...]).T.astype(BF16)
        values = dot_t(rows_in, wv[...])
        kv[me, c, key:key + part, :] = values[:, 0:128].astype(BF16)
        kv[me, c, key + part:, :] = jnp.concatenate(
            [values[k * fold:(k + 1) * fold, 128:] for k in range(128 // tail)], axis=1
        ).astype(BF16)

    def launch(c):
        pass_right(0, c)
        pass_left(0, c)
        go(copy_partner(me, 0, c))

    for start in range(strip, rows - strip, strip):
        mix(start)
    loads[0].wait()
    loads[1].wait()
    edge = (rows - part) // 2
    project(attn[edge:rows - edge, :], 0)
    launch(0)

    @pl.when(has_prev)
    def _():
        to_next.wait_recv()
        padded[0:HALO, :] = rms_norm(halo[0].astype(F32), gconv).astype(BF16).astype(F32)

    @pl.when(jnp.logical_not(has_prev))
    def _():
        padded[0:HALO, :] = jnp.zeros((HALO, width), F32)

    @pl.when(has_next)
    def _():
        to_prev.wait_recv()
        padded[HALO + rows:, :] = rms_norm(halo[1].astype(F32), gconv).astype(BF16).astype(F32)

    @pl.when(jnp.logical_not(has_next))
    def _():
        padded[HALO + rows:, :] = jnp.zeros((HALO, width), F32)

    mix(0)
    mix(rows - strip)
    project(jnp.concatenate([attn[0:edge, :], attn[rows - edge:, :]], axis=0), 1)
    launch(1)

    loads[2].wait()
    scale = math.log2(math.e) / math.sqrt(key)
    for h in range(HEADS):
        q_ref[h] = (dot(attn[...], wq[:, h * key:(h + 1) * key]) * scale).astype(BF16)

    lane = lax.broadcasted_iota(jnp.int32, (fold, 128), 1)

    def attend(pieces, initial, b):
        for k, (s, c) in enumerate(pieces):
            turned[b, :, k * part:(k + 1) * part] = kv[s, c, 0:key, :]
            stage[b, k * part:(k + 1) * part, 0:128] = kv[s, c, key:key + part, :]
            packed = kv[s, c, key + part:, :].astype(F32)
            for f in range(128 // tail):
                moved = packed if f == 0 else pltpu.roll(packed, 128 - f * tail, 1)
                base = k * part + f * fold
                stage[b, base:base + fold, 128:256] = jnp.where(lane < tail, moved, 1.0).astype(BF16)
        count = len(pieces) * part

        def score(h):
            return dot(q_ref[h], turned[b, :, 0:count])

        def soften(h, scores):
            best = jnp.broadcast_to(jnp.max(scores, axis=1, keepdims=True), (rows, 128))
            old = None
            if not initial:
                old = top[h]
                best = jnp.maximum(old, best)
            return jnp.exp2((scores - jnp.concatenate([best] * (count // 128), axis=1)).astype(BF16)), best, old

        def gather(h, weights, best, old):
            update = dot(weights, stage[b, 0:count, :])
            if initial:
                acc[h] = update
            else:
                factor = jnp.exp2(old - best)
                acc[h] = acc[h] * jnp.concatenate([factor] * (update.shape[1] // 128), axis=1) + update
            top[h] = best

        scores = score(0)
        held = None
        for h in range(HEADS):
            following = score(h + 1) if h + 1 < HEADS else None
            softened = soften(h, scores)
            if held is not None:
                gather(*held)
            held = (h,) + softened
            scores = following
        gather(*held)

    for c in range(PARTS):
        arrived(partner, c)
    waiting = ([(s, c) for s in (me, partner) for c in range(PARTS)], [])
    count = 1
    turn = 0

    def work(waiting, turn):
        for s, c in waiting[1]:
            arrived(s, c)
        attend(waiting[0] + waiting[1], turn == 0, turn % 2)

    for t in range(right_steps + (1 if opposite else 0)):
        last = t == right_steps
        for c in range(PARTS):
            places = []
            if not last or c < by_right:
                places.append(pos - 1 - t)
            if not last or c >= by_right:
                places.append(pos + 1 + t)
            for k, place in enumerate(places):
                slot = mine_at(place)
                arrived(slot, c)
                if not last:
                    (pass_right if k == 0 else pass_left)(t + 1, c)
                go(copy_partner(slot, count + k, c))
            work(waiting, turn)
            turn += 1
            waiting = ([(mine_at(p), c) for p in places], [(other_at(p), c) for p in places])
        count += 2
    work(waiting, turn)

    for pair in range(0, HEADS, 2):
        both = []
        for h in (pair, pair + 1):
            block = acc[h]
            both.append((block[:, :val] * (1.0 / block[:, val:val + 1])).astype(BF16))
        attended[:, pair * val:(pair + 2) * val] = jnp.concatenate(both, axis=1)

    loads[3].wait()
    band = rows // POOL
    member = lax.broadcasted_iota(jnp.int32, (band, rows), 1) // POOL
    pool = jnp.where(member == lax.broadcasted_iota(jnp.int32, (band, rows), 0), 1.0 / POOL, 0.0).astype(BF16)
    loads[4].wait()
    loads[5].wait()
    left = jnp.zeros((band, wl.shape[1]), F32)
    right = jnp.zeros((band, wr.shape[1]), F32)
    cols = 512 if width % 512 == 0 else width
    for start in range(0, width, cols):
        stop = start + cols
        block = (first[:, start:stop].astype(F32) + dot(attended[...], wo[:, start:stop])).astype(BF16)
        track_ref[:, start:stop] = block
        pooled = dot(pool, block).astype(BF16)
        left = left + dot(pooled, wl[start:stop, :])
        right = right + dot(pooled, wr[start:stop, :])
    track_out = pltpu.make_async_copy(track_ref, track_hbm, track_sem)
    track_out.start()
    own_left[...] = left.astype(BF16)
    right_land[me] = right.astype(BF16)

    left_next = send(own_left, left_halo.at[0], left_send.at[0], left_recv.at[0], after)
    left_prev = send(own_left, left_halo.at[1], left_send.at[1], left_recv.at[1], prev)

    @pl.when(has_next)
    def _():
        left_next.start()

    @pl.when(has_prev)
    def _():
        left_prev.start()

    def right_copy(step):
        return send(right_land.at[me], right_land.at[me], right_send.at[step], right_recv.at[me], lax.rem(me + step, n))

    @pl.loop(1, n)
    def _(step):
        right_copy(step).start()

    left_ext[...] = jnp.zeros(left_ext.shape, F32)
    left_ext[8:8 + band, :] = own_left[...].astype(F32)

    @pl.when(has_prev)
    def _():
        left_next.wait_recv()
        left_ext[7:8, :] = left_halo[0].astype(F32)[band - 1:band, :]

    @pl.when(has_next)
    def _():
        left_prev.wait_recv()
        left_ext[8 + band:9 + band, :] = left_halo[1].astype(F32)[0:1, :]

    @pl.loop(1, n)
    def _(step):
        slot = lax.rem(me + step, n)
        send(right_land.at[slot], right_land.at[slot], right_send.at[step], right_recv.at[slot], slot).wait_recv()

    @pl.when(has_next)
    def _():
        to_next.wait_send()
        left_next.wait_send()

    @pl.when(has_prev)
    def _():
        to_prev.wait_send()
        left_prev.wait_send()

    for copy in sent:
        copy.wait_send()

    @pl.loop(1, n)
    def _(step):
        right_copy(step).wait_send()

    track_out.wait()


def pair_kernel(
    track_in, left_ext, right_land, wp_hbm, track_out, pair_out,
    track, wp, right_all, act, pair, w_sem, track_sem, pair_sem,
):
    load = pltpu.make_async_copy(wp_hbm, wp, w_sem)
    load.start()
    track_load = pltpu.make_async_copy(track_in, track, track_sem)
    track_load.start()
    columns, channels = right_all.shape
    band = pair.shape[0]
    right_all[...] = right_land[...].astype(F32).reshape(columns, channels)
    column = lax.broadcasted_iota(jnp.int32, (columns, channels), 0)

    @pl.loop(0, band + 2)
    def _(i):
        product = (left_ext[pl.ds(i + 7, 1), :] * right_all[...]).astype(BF16).astype(F32)
        active = jax.nn.gelu(product)
        act[i, :, 0:channels] = jnp.where(column == 0, 0.0, pltpu.roll(active, 1, 0)).astype(BF16)
        act[i, :, channels:2 * channels] = active.astype(BF16)
        act[i, :, 2 * channels:] = jnp.where(column == columns - 1, 0.0, pltpu.roll(active, columns - 1, 0)).astype(BF16)

    span = 3 * channels
    track_load.wait()
    track_store = pltpu.make_async_copy(track, track_out, track_sem)
    track_store.start()
    load.wait()

    def store(i):
        return pltpu.make_async_copy(pair.at[i], pair_out.at[i], pair_sem.at[i])

    @pl.loop(0, band)
    def _(i):
        total = (left_ext[pl.ds(i + 8, 1), :] * right_all[...]).astype(BF16).astype(F32)
        for a in range(3):
            total = total + dot(act[i + a], wp[a * span:(a + 1) * span, :])
        pair[i] = total.astype(BF16)
        store(i).start()

    track_store.wait()

    @pl.loop(0, band)
    def _(i):
        store(i).wait()


def solution(mesh):
    n = mesh.shape["seq"]

    def local(sequence, gain_conv, conv_weight, gain_attn, w_query, w_key, w_value, w_out, w_left, w_right, w_pair):
        rows, width = sequence.shape
        key, val = w_key.shape[1], w_value.shape[1]
        channels = w_left.shape[1]
        band = rows // POOL
        columns = n * band
        chips = n // 2
        value_lanes = (val // 128 + 1) * 128
        tail_rows = rows // PARTS // (128 // (val - 128))
        taps = w_pair.reshape(-1, channels)
        weights = (w_query, w_key, w_value.T, w_out, w_left, w_right)
        anyspace = pl.BlockSpec(memory_space=pl.ANY)
        vmem = pl.BlockSpec(memory_space=pltpu.VMEM)
        dma = pltpu.SemaphoreType.DMA
        steps = max(chips // 2, 1)
        track, left, right = pl.pallas_call(
            functools.partial(kernel, n),
            out_shape=(
                jax.ShapeDtypeStruct((rows, width), BF16),
                jax.ShapeDtypeStruct((band + 16, channels), F32),
                jax.ShapeDtypeStruct((n, band, channels), BF16),
            ),
            in_specs=[vmem] * 2 + [anyspace] * 8,
            out_specs=(anyspace, vmem, vmem),
            scratch_shapes=[pltpu.VMEM((2, width), F32)]
            + [pltpu.VMEM(w.shape, BF16) for w in weights]
            + [
                pltpu.VMEM((rows, width), BF16),
                pltpu.VMEM((2, HALO, width), BF16),
                pltpu.VMEM((rows + 2 * HALO, width), F32),
                pltpu.VMEM((rows, width), BF16),
                pltpu.VMEM((rows, width), BF16),
                pltpu.VMEM((HEADS, rows, key), BF16),
                pltpu.VMEM((n, PARTS, key + rows // PARTS + tail_rows, 128), BF16),
                pltpu.VMEM((HEADS, rows, value_lanes), F32),
                pltpu.VMEM((HEADS, rows, 128), F32),
                pltpu.VMEM((rows, HEADS * val), BF16),
                pltpu.VMEM((band, channels), BF16),
                pltpu.VMEM((2, band, channels), BF16),
                pltpu.VMEM((2, key, 4 * (rows // PARTS)), BF16),
                pltpu.VMEM((2, 4 * (rows // PARTS), value_lanes), BF16),
                dma((len(weights) + 2,)),
                dma(()),
                dma((2,)),
                dma((2,)),
                dma((steps + 1, PARTS)),
                dma((steps + 1, PARTS)),
                dma((chips + 1, PARTS)),
                dma((n, PARTS)),
                dma((2,)),
                dma((2,)),
                dma((n,)),
                dma((n,)),
            ],
            compiler_params=pltpu.CompilerParams(
                collective_id=0, has_side_effects=True, vmem_limit_bytes=60 * 1024 * 1024
            ),
        )(sequence, conv_weight, gain_conv, gain_attn, *weights)
        return pl.pallas_call(
            pair_kernel,
            out_shape=(
                jax.ShapeDtypeStruct((rows, width), BF16),
                jax.ShapeDtypeStruct((band, columns, channels), BF16),
            ),
            in_specs=[anyspace, vmem, vmem, anyspace],
            out_specs=(anyspace, anyspace),
            scratch_shapes=[
                pltpu.VMEM((rows, width), BF16),
                pltpu.VMEM(taps.shape, BF16),
                pltpu.VMEM((columns, channels), F32),
                pltpu.VMEM((band + 2, columns, 3 * channels), BF16),
                pltpu.VMEM((band, columns, channels), BF16),
                dma(()),
                dma(()),
                dma((band,)),
            ],
            compiler_params=pltpu.CompilerParams(vmem_limit_bytes=60 * 1024 * 1024),
        )(track, left, right, taps)

    placed = (P(("groups", "seq"), None),) + (P(),) * 10
    return jax.shard_map(
        local,
        mesh=mesh,
        in_specs=placed,
        out_specs=(P(("groups", "seq"), None), P(("groups", "seq"), None, None)),
        check_vma=False,
    )
```

```python
import functools
import math

import jax
import jax.numpy as jnp
from jax import lax
from jax.experimental import pallas as pl
from jax.experimental.pallas import tpu as pltpu
from jax.sharding import PartitionSpec as P

HEADS = 8
POOL = 16
HALO = 16
PARTS = 2
SPLIT = 1
F32 = jnp.float32
BF16 = jnp.bfloat16


def dot(a, b):
    return jnp.dot(a, b, preferred_element_type=F32)


def dot_t(a, b):
    return lax.dot_general(a, b, (((1,), (1,)), ((), ())), preferred_element_type=F32)


def rms_norm(values, gain):
    scale = lax.rsqrt(jnp.mean(values * values, axis=-1, keepdims=True) + 1e-06)
    return values * scale * gain


def kernel(
    n,
    seq_ref, conv_ref,
    gconv_hbm, gattn_hbm, wq_hbm, wk_hbm, wv_hbm, wo_hbm, wl_hbm, wr_hbm,
    track_hbm, left_ext, right_land,
    gains, wq, wk, wv, wo, wl, wr, track_ref,
    halo, padded, first, attn, q_ref, kv, acc, top, attended,
    own_left, left_halo, turned, stage,
    w_sem, track_sem, halo_send, halo_recv, r_send, l_send, p_send, kv_recv,
    left_send, left_recv, right_send, right_recv,
):
    rows, width = seq_ref.shape
    key = wk.shape[1]
    val = wv.shape[0]
    taps = conv_ref.shape[0]
    reach = taps // 2
    part = rows // PARTS
    chips = n // 2
    half = (chips + 1) // 2
    me = lax.axis_index("seq")
    chip = me // 2
    core = me % 2
    partner = chip * 2 + (1 - core)
    pos = jnp.where(chip % 2 == 0, chip // 2, chips - 1 - chip // 2)

    def chip_at(place):
        place = lax.rem(place + 2 * chips, chips)
        return jnp.where(place < half, 2 * place, 2 * (chips - 1 - place) + 1)

    def mine_at(place):
        return chip_at(place) * 2 + core

    def other_at(place):
        return chip_at(place) * 2 + (1 - core)

    barrier = pltpu.get_barrier_semaphore()

    @pl.loop(1, n)
    def _(step):
        pl.semaphore_signal(barrier, inc=1, device_id={"seq": lax.rem(me + step, n)})

    pairs = (
        (wk_hbm, wk), (wv_hbm, wv), (wq_hbm, wq), (wo_hbm, wo), (wl_hbm, wl), (wr_hbm, wr),
        (gconv_hbm, gains.at[0]), (gattn_hbm, gains.at[1]),
    )
    loads = [pltpu.make_async_copy(s, d, w_sem.at[i]) for i, (s, d) in enumerate(pairs)]
    for load in loads[6:] + loads[:6]:
        load.start()

    def send(src, dst, ssem, rsem, to):
        return pltpu.make_async_remote_copy(
            src_ref=src, dst_ref=dst, send_sem=ssem, recv_sem=rsem, device_id={"seq": to}
        )

    has_prev = me > 0
    has_next = me < n - 1
    prev = lax.rem(me + n - 1, n)
    after = lax.rem(me + 1, n)
    to_next = send(seq_ref.at[pl.ds(rows - HALO, HALO)], halo.at[0], halo_send.at[0], halo_recv.at[0], after)
    to_prev = send(seq_ref.at[pl.ds(0, HALO)], halo.at[1], halo_send.at[1], halo_recv.at[1], prev)

    loads[6].wait()
    loads[7].wait()
    gconv = gains[0:1, :]
    strip = 32
    for start in range(0, rows, strip):
        values = seq_ref[start:start + strip, :].astype(F32)
        padded[HALO + start:HALO + start + strip, :] = rms_norm(values, gconv).astype(BF16).astype(F32)

    pl.semaphore_wait(barrier, n - 1)

    @pl.when(has_next)
    def _():
        to_next.start()

    @pl.when(has_prev)
    def _():
        to_prev.start()

    gattn = gains[1:2, :]

    def mix(start):
        total = seq_ref[start:start + strip, :].astype(F32)
        conv = jnp.zeros((strip, width), F32)
        for tap in range(taps):
            base = HALO + start + tap - reach
            conv = conv + conv_ref[tap:tap + 1, :] * padded[base:base + strip, :]
        one = (total + conv).astype(BF16)
        first[start:start + strip, :] = one
        attn[start:start + strip, :] = rms_norm(one.astype(F32), gattn).astype(BF16)

    right_steps = (chips - 1) // 2
    opposite = chips % 2 == 0
    to_right = mine_at(pos + 1)
    to_left = mine_at(pos - 1)
    by_right = PARTS // 2

    size = kv.shape[2] // SPLIT

    def piece(slot, c, u):
        return kv.at[slot, c, pl.ds(u * size, size)]

    def move(slot, c, u, ssem, to):
        return send(piece(slot, c, u), piece(slot, c, u), ssem, kv_recv.at[slot, c, u], to)

    def copy_right(t, c, u):
        return move(mine_at(pos - t), c, u, r_send.at[t, c, u], to_right)

    def copy_left(t, c, u):
        return move(mine_at(pos + t), c, u, l_send.at[t, c, u], to_left)

    def copy_partner(slot, count, c, u):
        return move(slot, c, u, p_send.at[count, c, u], partner)

    def arrived(slot, c, u):
        move(slot, c, u, p_send.at[0, c, u], partner).wait_recv()

    sent = []

    def go(copy):
        copy.start()
        sent.append(copy)

    def pass_right(t, c, u):
        if t < right_steps or (opposite and t == right_steps and c < by_right):
            go(copy_right(t, c, u))

    def pass_left(t, c, u):
        if t < right_steps or (opposite and t == right_steps and c >= by_right):
            go(copy_left(t, c, u))

    tail = val - 128
    fold = part // (128 // tail)

    def project(rows_in, c):
        kv[me, c, 0:key, :] = dot(rows_in, wk[...]).T.astype(BF16)
        values = dot_t(rows_in, wv[...])
        kv[me, c, key:key + part, :] = values[:, 0:128].astype(BF16)
        kv[me, c, key + part:, :] = jnp.concatenate(
            [values[k * fold:(k + 1) * fold, 128:] for k in range(128 // tail)], axis=1
        ).astype(BF16)

    def launch(c):
        for u in range(SPLIT):
            pass_right(0, c, u)
            pass_left(0, c, u)
        for u in range(SPLIT):
            go(copy_partner(me, 0, c, u))

    for start in range(strip, rows - strip, strip):
        mix(start)
    loads[0].wait()
    loads[1].wait()
    edge = (rows - part) // 2
    project(attn[edge:rows - edge, :], 0)
    launch(0)

    @pl.when(has_prev)
    def _():
        to_next.wait_recv()
        padded[0:HALO, :] = rms_norm(halo[0].astype(F32), gconv).astype(BF16).astype(F32)

    @pl.when(jnp.logical_not(has_prev))
    def _():
        padded[0:HALO, :] = jnp.zeros((HALO, width), F32)

    @pl.when(has_next)
    def _():
        to_prev.wait_recv()
        padded[HALO + rows:, :] = rms_norm(halo[1].astype(F32), gconv).astype(BF16).astype(F32)

    @pl.when(jnp.logical_not(has_next))
    def _():
        padded[HALO + rows:, :] = jnp.zeros((HALO, width), F32)

    mix(0)
    mix(rows - strip)
    project(jnp.concatenate([attn[0:edge, :], attn[rows - edge:, :]], axis=0), 1)
    launch(1)

    loads[2].wait()
    scale = math.log2(math.e) / math.sqrt(key)
    for h in range(HEADS):
        q_ref[h] = (dot(attn[...], wq[:, h * key:(h + 1) * key]) * scale).astype(BF16)

    lane = lax.broadcasted_iota(jnp.int32, (fold, 128), 1)

    def attend(pieces, initial, b, between):
        for k, (s, c) in enumerate(pieces):
            turned[b, :, k * part:(k + 1) * part] = kv[s, c, 0:key, :]
            stage[b, k * part:(k + 1) * part, 0:128] = kv[s, c, key:key + part, :]
            packed = kv[s, c, key + part:, :].astype(F32)
            for f in range(128 // tail):
                moved = packed if f == 0 else pltpu.roll(packed, 128 - f * tail, 1)
                base = k * part + f * fold
                stage[b, base:base + fold, 128:256] = jnp.where(lane < tail, moved, 1.0).astype(BF16)
        count = len(pieces) * part

        def score(h):
            return dot(q_ref[h], turned[b, :, 0:count])

        def soften(h, scores):
            best = jnp.broadcast_to(jnp.max(scores, axis=1, keepdims=True), (rows, 128))
            old = None
            if not initial:
                old = top[h]
                best = jnp.maximum(old, best)
            return jnp.exp2((scores - jnp.concatenate([best] * (count // 128), axis=1)).astype(BF16)), best, old

        def gather(h, weights, best, old):
            update = dot(weights, stage[b, 0:count, :])
            if initial:
                acc[h] = update
            else:
                factor = jnp.exp2(old - best)
                acc[h] = acc[h] * jnp.concatenate([factor] * (update.shape[1] // 128), axis=1) + update
            top[h] = best

        scores = score(0)
        held = None
        for h in range(HEADS):
            following = score(h + 1) if h + 1 < HEADS else None
            softened = soften(h, scores)
            if held is not None:
                gather(*held)
            held = (h,) + softened
            scores = following
            if h in between:
                between[h]()
        gather(*held)

    for c in range(PARTS):
        for u in range(SPLIT):
            arrived(partner, c, u)
    waiting = ([(s, c) for s in (me, partner) for c in range(PARTS)], [])
    count = 1
    turn = 0

    def work(waiting, turn, between):
        for s, c in waiting[1]:
            for u in range(SPLIT):
                arrived(s, c, u)
        attend(waiting[0] + waiting[1], turn == 0, turn % 2, between)

    def relay(t, c, u, places, count):
        for k, place in enumerate(places):
            slot = mine_at(place)
            arrived(slot, c, u)
            if t < right_steps:
                (pass_right if k == 0 else pass_left)(t + 1, c, u)
            go(copy_partner(slot, count + k, c, u))

    for t in range(right_steps + (1 if opposite else 0)):
        last = t == right_steps
        for c in range(PARTS):
            places = []
            if not last or c < by_right:
                places.append(pos - 1 - t)
            if not last or c >= by_right:
                places.append(pos + 1 + t)
            relay(t, c, 0, places, count)
            work(waiting, turn, {
                u * HEADS // SPLIT - 1: functools.partial(relay, t, c, u, places, count) for u in range(1, SPLIT)
            })
            turn += 1
            waiting = ([(mine_at(p), c) for p in places], [(other_at(p), c) for p in places])
        count += 2
    work(waiting, turn, {})

    for pair in range(0, HEADS, 2):
        both = []
        for h in (pair, pair + 1):
            block = acc[h]
            both.append((block[:, :val] * (1.0 / block[:, val:val + 1])).astype(BF16))
        attended[:, pair * val:(pair + 2) * val] = jnp.concatenate(both, axis=1)

    loads[3].wait()
    band = rows // POOL
    member = lax.broadcasted_iota(jnp.int32, (band, rows), 1) // POOL
    pool = jnp.where(member == lax.broadcasted_iota(jnp.int32, (band, rows), 0), 1.0 / POOL, 0.0).astype(BF16)
    loads[4].wait()
    loads[5].wait()
    left = jnp.zeros((band, wl.shape[1]), F32)
    right = jnp.zeros((band, wr.shape[1]), F32)
    cols = 512 if width % 512 == 0 else width
    for start in range(0, width, cols):
        stop = start + cols
        block = (first[:, start:stop].astype(F32) + dot(attended[...], wo[:, start:stop])).astype(BF16)
        track_ref[:, start:stop] = block
        pooled = dot(pool, block).astype(BF16)
        left = left + dot(pooled, wl[start:stop, :])
        right = right + dot(pooled, wr[start:stop, :])
    track_out = pltpu.make_async_copy(track_ref, track_hbm, track_sem)
    track_out.start()
    own_left[...] = left.astype(BF16)
    right_land[me] = right.astype(BF16)

    left_next = send(own_left, left_halo.at[0], left_send.at[0], left_recv.at[0], after)
    left_prev = send(own_left, left_halo.at[1], left_send.at[1], left_recv.at[1], prev)

    @pl.when(has_next)
    def _():
        left_next.start()

    @pl.when(has_prev)
    def _():
        left_prev.start()

    def right_copy(step):
        return send(right_land.at[me], right_land.at[me], right_send.at[step], right_recv.at[me], lax.rem(me + step, n))

    @pl.loop(1, n)
    def _(step):
        right_copy(step).start()

    left_ext[...] = jnp.zeros(left_ext.shape, F32)
    left_ext[8:8 + band, :] = own_left[...].astype(F32)

    @pl.when(has_prev)
    def _():
        left_next.wait_recv()
        left_ext[7:8, :] = left_halo[0].astype(F32)[band - 1:band, :]

    @pl.when(has_next)
    def _():
        left_prev.wait_recv()
        left_ext[8 + band:9 + band, :] = left_halo[1].astype(F32)[0:1, :]

    @pl.loop(1, n)
    def _(step):
        slot = lax.rem(me + step, n)
        send(right_land.at[slot], right_land.at[slot], right_send.at[step], right_recv.at[slot], slot).wait_recv()

    @pl.when(has_next)
    def _():
        to_next.wait_send()
        left_next.wait_send()

    @pl.when(has_prev)
    def _():
        to_prev.wait_send()
        left_prev.wait_send()

    for copy in sent:
        copy.wait_send()

    @pl.loop(1, n)
    def _(step):
        right_copy(step).wait_send()

    track_out.wait()


def pair_kernel(
    track_in, left_ext, right_land, wp_hbm, track_out, pair_out,
    track, wp, wide, right_all, act, pair, w_sem, track_sem, pair_sem,
):
    load = pltpu.make_async_copy(wp_hbm, wp, w_sem)
    load.start()
    track_load = pltpu.make_async_copy(track_in, track, track_sem)
    track_load.start()
    columns, channels = right_all.shape
    band = pair.shape[0]
    span = 3 * channels
    right_all[...] = right_land[...].astype(F32).reshape(columns, channels)
    column = lax.broadcasted_iota(jnp.int32, (columns, channels), 0)

    def product(i):
        return (left_ext[i + 7:i + 8, :] * right_all[...]).astype(BF16).astype(F32)

    def activate(i):
        active = jax.nn.gelu(product(i))
        act[i, :, 0:channels] = jnp.where(column == 0, 0.0, pltpu.roll(active, 1, 0)).astype(BF16)
        act[i, :, channels:2 * channels] = active.astype(BF16)
        act[i, :, 2 * channels:] = jnp.where(column == columns - 1, 0.0, pltpu.roll(active, columns - 1, 0)).astype(BF16)

    for i in range(4):
        activate(i)

    load.wait()
    zero = jnp.zeros((span, channels), BF16)
    for r in range(4):
        for o in range(2):
            tap = r - o
            wide[r * span:(r + 1) * span, o * channels:(o + 1) * channels] = (
                wp[tap * span:(tap + 1) * span, :] if 0 <= tap <= 2 else zero
            )
    track_load.wait()
    track_store = pltpu.make_async_copy(track, track_out, track_sem)
    track_store.start()

    def store(i):
        return pltpu.make_async_copy(pair.at[i], pair_out.at[i], pair_sem.at[i])

    for i in range(0, band, 2):
        both = dot(jnp.concatenate([act[i + r] for r in range(4)], axis=1), wide[...])
        for k in (i + 4, i + 5):
            if k < band + 2:
                activate(k)
        for o in range(2):
            pair[i + o] = (product(i + o + 1) + both[:, o * channels:(o + 1) * channels]).astype(BF16)
            store(i + o).start()

    track_store.wait()
    for i in range(band):
        store(i).wait()


def solution(mesh):
    n = mesh.shape["seq"]

    def local(sequence, gain_conv, conv_weight, gain_attn, w_query, w_key, w_value, w_out, w_left, w_right, w_pair):
        rows, width = sequence.shape
        key, val = w_key.shape[1], w_value.shape[1]
        channels = w_left.shape[1]
        band = rows // POOL
        columns = n * band
        chips = n // 2
        value_lanes = (val // 128 + 1) * 128
        tail_rows = rows // PARTS // (128 // (val - 128))
        taps = w_pair.reshape(-1, channels)
        weights = (w_query, w_key, w_value.T, w_out, w_left, w_right)
        anyspace = pl.BlockSpec(memory_space=pl.ANY)
        vmem = pl.BlockSpec(memory_space=pltpu.VMEM)
        dma = pltpu.SemaphoreType.DMA
        steps = max(chips // 2, 1)
        track, left, right = pl.pallas_call(
            functools.partial(kernel, n),
            out_shape=(
                jax.ShapeDtypeStruct((rows, width), BF16),
                jax.ShapeDtypeStruct((band + 16, channels), F32),
                jax.ShapeDtypeStruct((n, band, channels), BF16),
            ),
            in_specs=[vmem] * 2 + [anyspace] * 8,
            out_specs=(anyspace, vmem, vmem),
            scratch_shapes=[pltpu.VMEM((2, width), F32)]
            + [pltpu.VMEM(w.shape, BF16) for w in weights]
            + [
                pltpu.VMEM((rows, width), BF16),
                pltpu.VMEM((2, HALO, width), BF16),
                pltpu.VMEM((rows + 2 * HALO, width), F32),
                pltpu.VMEM((rows, width), BF16),
                pltpu.VMEM((rows, width), BF16),
                pltpu.VMEM((HEADS, rows, key), BF16),
                pltpu.VMEM((n, PARTS, key + rows // PARTS + tail_rows, 128), BF16),
                pltpu.VMEM((HEADS, rows, value_lanes), F32),
                pltpu.VMEM((HEADS, rows, 128), F32),
                pltpu.VMEM((rows, HEADS * val), BF16),
                pltpu.VMEM((band, channels), BF16),
                pltpu.VMEM((2, band, channels), BF16),
                pltpu.VMEM((2, key, 4 * (rows // PARTS)), BF16),
                pltpu.VMEM((2, 4 * (rows // PARTS), value_lanes), BF16),
                dma((len(weights) + 2,)),
                dma(()),
                dma((2,)),
                dma((2,)),
                dma((steps + 1, PARTS, SPLIT)),
                dma((steps + 1, PARTS, SPLIT)),
                dma((chips + 1, PARTS, SPLIT)),
                dma((n, PARTS, SPLIT)),
                dma((2,)),
                dma((2,)),
                dma((n,)),
                dma((n,)),
            ],
            compiler_params=pltpu.CompilerParams(
                collective_id=0, has_side_effects=True, vmem_limit_bytes=60 * 1024 * 1024
            ),
        )(sequence, conv_weight, gain_conv, gain_attn, *weights)
        return pl.pallas_call(
            pair_kernel,
            out_shape=(
                jax.ShapeDtypeStruct((rows, width), BF16),
                jax.ShapeDtypeStruct((band, columns, channels), BF16),
            ),
            in_specs=[anyspace, vmem, vmem, anyspace],
            out_specs=(anyspace, anyspace),
            scratch_shapes=[
                pltpu.VMEM((rows, width), BF16),
                pltpu.VMEM(taps.shape, BF16),
                pltpu.VMEM((12 * channels, 2 * channels), BF16),
                pltpu.VMEM((columns, channels), F32),
                pltpu.VMEM((band + 2, columns, 3 * channels), BF16),
                pltpu.VMEM((band, columns, channels), BF16),
                dma(()),
                dma(()),
                dma((band,)),
            ],
            compiler_params=pltpu.CompilerParams(vmem_limit_bytes=60 * 1024 * 1024),
        )(track, left, right, taps)

    placed = (P(("groups", "seq"), None),) + (P(),) * 10
    return jax.shard_map(
        local,
        mesh=mesh,
        in_specs=placed,
        out_specs=(P(("groups", "seq"), None), P(("groups", "seq"), None, None)),
        check_vma=False,
    )
```

```python
import functools
import math

import jax
import jax.numpy as jnp
from jax import lax
from jax.experimental import pallas as pl
from jax.experimental.pallas import tpu as pltpu
from jax.sharding import PartitionSpec as P

HEADS = 8
POOL = 16
HALO = 16
PARTS = 2
SPLIT = 1
F32 = jnp.float32
BF16 = jnp.bfloat16


def dot(a, b):
    return jnp.dot(a, b, preferred_element_type=F32)


def dot_t(a, b):
    return lax.dot_general(a, b, (((1,), (1,)), ((), ())), preferred_element_type=F32)


def rms_norm(values, gain):
    scale = lax.rsqrt(jnp.mean(values * values, axis=-1, keepdims=True) + 1e-06)
    return values * scale * gain


def kernel(
    n,
    seq_ref, conv_ref,
    gconv_hbm, gattn_hbm, wq_hbm, wk_hbm, wv_hbm, wo_hbm, wl_hbm, wr_hbm,
    track_hbm, left_ext, right_land,
    gains, wq, wk, wv, wo, wlr, folded, track_ref,
    halo, padded, first, attn, q_ref, kv, acc, top, attended,
    own_left, left_halo, turned, stage,
    w_sem, track_sem, halo_send, halo_recv, r_send, l_send, p_send, kv_recv,
    left_send, left_recv, right_send, right_recv,
):
    rows, width = seq_ref.shape
    key = wk.shape[1]
    val = wv.shape[0]
    taps = conv_ref.shape[0]
    reach = taps // 2
    part = rows // PARTS
    chips = n // 2
    half = (chips + 1) // 2
    me = lax.axis_index("seq")
    chip = me // 2
    core = me % 2
    partner = chip * 2 + (1 - core)
    pos = jnp.where(chip % 2 == 0, chip // 2, chips - 1 - chip // 2)

    def chip_at(place):
        place = lax.rem(place + 2 * chips, chips)
        return jnp.where(place < half, 2 * place, 2 * (chips - 1 - place) + 1)

    def mine_at(place):
        return chip_at(place) * 2 + core

    def other_at(place):
        return chip_at(place) * 2 + (1 - core)

    barrier = pltpu.get_barrier_semaphore()

    @pl.loop(1, n)
    def _(step):
        pl.semaphore_signal(barrier, inc=1, device_id={"seq": lax.rem(me + step, n)})

    pairs = (
        (wk_hbm, wk), (wv_hbm, wv), (wq_hbm, wq), (wo_hbm, wo),
        (wl_hbm, wlr.at[:, pl.ds(0, wlr.shape[1] // 2)]),
        (wr_hbm, wlr.at[:, pl.ds(wlr.shape[1] // 2, wlr.shape[1] // 2)]),
        (gconv_hbm, gains.at[0]), (gattn_hbm, gains.at[1]),
    )
    loads = [pltpu.make_async_copy(s, d, w_sem.at[i]) for i, (s, d) in enumerate(pairs)]
    for load in loads[6:] + loads[:3] + loads[4:6] + loads[3:4]:
        load.start()

    def send(src, dst, ssem, rsem, to):
        return pltpu.make_async_remote_copy(
            src_ref=src, dst_ref=dst, send_sem=ssem, recv_sem=rsem, device_id={"seq": to}
        )

    has_prev = me > 0
    has_next = me < n - 1
    prev = lax.rem(me + n - 1, n)
    after = lax.rem(me + 1, n)
    to_next = send(seq_ref.at[pl.ds(rows - HALO, HALO)], halo.at[0], halo_send.at[0], halo_recv.at[0], after)
    to_prev = send(seq_ref.at[pl.ds(0, HALO)], halo.at[1], halo_send.at[1], halo_recv.at[1], prev)

    loads[6].wait()
    loads[7].wait()
    gconv = gains[0:1, :]
    strip = 32
    for start in range(0, rows, strip):
        values = seq_ref[start:start + strip, :].astype(F32)
        padded[HALO + start:HALO + start + strip, :] = rms_norm(values, gconv).astype(BF16).astype(F32)

    pl.semaphore_wait(barrier, n - 1)

    @pl.when(has_next)
    def _():
        to_next.start()

    @pl.when(has_prev)
    def _():
        to_prev.start()

    gattn = gains[1:2, :]

    def mix(start):
        total = seq_ref[start:start + strip, :].astype(F32)
        conv = jnp.zeros((strip, width), F32)
        for tap in range(taps):
            base = HALO + start + tap - reach
            conv = conv + conv_ref[tap:tap + 1, :] * padded[base:base + strip, :]
        one = (total + conv).astype(BF16)
        first[start:start + strip, :] = one
        attn[start:start + strip, :] = rms_norm(one.astype(F32), gattn).astype(BF16)

    right_steps = (chips - 1) // 2
    opposite = chips % 2 == 0
    to_right = mine_at(pos + 1)
    to_left = mine_at(pos - 1)
    by_right = PARTS // 2

    size = kv.shape[2] // SPLIT

    def piece(slot, c, u):
        return kv.at[slot, c, pl.ds(u * size, size)]

    def move(slot, c, u, ssem, to):
        return send(piece(slot, c, u), piece(slot, c, u), ssem, kv_recv.at[slot, c, u], to)

    def copy_right(t, c, u):
        return move(mine_at(pos - t), c, u, r_send.at[t, c, u], to_right)

    def copy_left(t, c, u):
        return move(mine_at(pos + t), c, u, l_send.at[t, c, u], to_left)

    def copy_partner(slot, count, c, u):
        return move(slot, c, u, p_send.at[count, c, u], partner)

    def arrived(slot, c, u):
        move(slot, c, u, p_send.at[0, c, u], partner).wait_recv()

    sent = []

    def go(copy):
        copy.start()
        sent.append(copy)

    def pass_right(t, c, u):
        if t < right_steps or (opposite and t == right_steps and c < by_right):
            go(copy_right(t, c, u))

    def pass_left(t, c, u):
        if t < right_steps or (opposite and t == right_steps and c >= by_right):
            go(copy_left(t, c, u))

    tail = val - 128
    fold = part // (128 // tail)

    def project(rows_in, c):
        kv[me, c, 0:key, :] = dot(rows_in, wk[...]).T.astype(BF16)
        values = dot_t(rows_in, wv[...])
        kv[me, c, key:key + part, :] = values[:, 0:128].astype(BF16)
        kv[me, c, key + part:, :] = jnp.concatenate(
            [values[k * fold:(k + 1) * fold, 128:] for k in range(128 // tail)], axis=1
        ).astype(BF16)

    def launch(c):
        for u in range(SPLIT):
            pass_right(0, c, u)
            pass_left(0, c, u)
        for u in range(SPLIT):
            go(copy_partner(me, 0, c, u))

    for start in range(strip, rows - strip, strip):
        mix(start)
    loads[0].wait()
    loads[1].wait()
    edge = (rows - part) // 2
    project(attn[edge:rows - edge, :], 0)
    launch(0)

    @pl.when(has_prev)
    def _():
        to_next.wait_recv()
        padded[0:HALO, :] = rms_norm(halo[0].astype(F32), gconv).astype(BF16).astype(F32)

    @pl.when(jnp.logical_not(has_prev))
    def _():
        padded[0:HALO, :] = jnp.zeros((HALO, width), F32)

    @pl.when(has_next)
    def _():
        to_prev.wait_recv()
        padded[HALO + rows:, :] = rms_norm(halo[1].astype(F32), gconv).astype(BF16).astype(F32)

    @pl.when(jnp.logical_not(has_next))
    def _():
        padded[HALO + rows:, :] = jnp.zeros((HALO, width), F32)

    mix(0)
    mix(rows - strip)
    project(jnp.concatenate([attn[0:edge, :], attn[rows - edge:, :]], axis=0), 1)
    launch(1)

    loads[2].wait()
    scale = math.log2(math.e) / math.sqrt(key)
    for h in range(HEADS):
        q_ref[h] = (dot(attn[...], wq[:, h * key:(h + 1) * key]) * scale).astype(BF16)

    lane = lax.broadcasted_iota(jnp.int32, (fold, 128), 1)

    def attend(pieces, initial, b, between):
        for k, (s, c) in enumerate(pieces):
            turned[b, :, k * part:(k + 1) * part] = kv[s, c, 0:key, :]
            stage[b, k * part:(k + 1) * part, 0:128] = kv[s, c, key:key + part, :]
            packed = kv[s, c, key + part:, :].astype(F32)
            for f in range(128 // tail):
                moved = packed if f == 0 else pltpu.roll(packed, 128 - f * tail, 1)
                base = k * part + f * fold
                stage[b, base:base + fold, 128:256] = jnp.where(lane < tail, moved, 1.0).astype(BF16)
        count = len(pieces) * part

        def score(h):
            return dot(q_ref[h], turned[b, :, 0:count])

        def soften(h, scores):
            best = jnp.broadcast_to(jnp.max(scores, axis=1, keepdims=True), (rows, 128))
            old = None
            if not initial:
                old = top[h]
                best = jnp.maximum(old, best)
            return jnp.exp2((scores - jnp.concatenate([best] * (count // 128), axis=1)).astype(BF16)), best, old

        def gather(h, weights, best, old):
            update = dot(weights, stage[b, 0:count, :])
            if initial:
                acc[h] = update
            else:
                factor = jnp.exp2(old - best)
                acc[h] = acc[h] * jnp.concatenate([factor] * (update.shape[1] // 128), axis=1) + update
            top[h] = best

        scores = score(0)
        held = None
        for h in range(HEADS):
            following = score(h + 1) if h + 1 < HEADS else None
            softened = soften(h, scores)
            if held is not None:
                gather(*held)
            held = (h,) + softened
            scores = following
            if h in between:
                between[h]()
        gather(*held)

    for c in range(PARTS):
        for u in range(SPLIT):
            arrived(partner, c, u)
    waiting = ([(s, c) for s in (me, partner) for c in range(PARTS)], [])
    count = 1
    turn = 0

    band = rows // POOL
    member = lax.broadcasted_iota(jnp.int32, (band, rows), 1) // POOL
    pool = jnp.where(member == lax.broadcasted_iota(jnp.int32, (band, rows), 0), 1.0 / POOL, 0.0).astype(BF16)
    base = []
    deep = 256 if wo.shape[0] % 256 == 0 else wo.shape[0]

    def fold_out(turn):
        if turn == 0:
            loads[4].wait()
            loads[5].wait()
            base.append(dot(dot(pool, first[...]).astype(BF16), wlr[...]))
        elif turn == 1:
            loads[3].wait()
        if turn:
            if turn <= wo.shape[0] // deep:
                k = turn - 1
                folded[k * deep:(k + 1) * deep, :] = dot(wo[k * deep:(k + 1) * deep, :], wlr[...]).astype(BF16)

    def work(waiting, turn, between):
        for s, c in waiting[1]:
            for u in range(SPLIT):
                arrived(s, c, u)
        attend(waiting[0] + waiting[1], turn == 0, turn % 2, between)

    def relay(t, c, u, places, count):
        for k, place in enumerate(places):
            slot = mine_at(place)
            arrived(slot, c, u)
            if t < right_steps:
                (pass_right if k == 0 else pass_left)(t + 1, c, u)
            go(copy_partner(slot, count + k, c, u))

    for t in range(right_steps + (1 if opposite else 0)):
        last = t == right_steps
        for c in range(PARTS):
            places = []
            if not last or c < by_right:
                places.append(pos - 1 - t)
            if not last or c >= by_right:
                places.append(pos + 1 + t)
            relay(t, c, 0, places, count)
            work(waiting, turn, {
                u * HEADS // SPLIT - 1: functools.partial(relay, t, c, u, places, count) for u in range(1, SPLIT)
            })
            fold_out(turn)
            turn += 1
            waiting = ([(mine_at(p), c) for p in places], [(other_at(p), c) for p in places])
        count += 2
    for later in range(turn, 1 - (-(wo.shape[0] // deep) // 1)):
        fold_out(later)
    work(waiting, turn, {})

    for pair in range(0, HEADS, 2):
        both = []
        for h in (pair, pair + 1):
            block = acc[h]
            both.append((block[:, :val] * (1.0 / block[:, val:val + 1])).astype(BF16))
        attended[:, pair * val:(pair + 2) * val] = jnp.concatenate(both, axis=1)

    pooled = dot(pool, attended[...]).astype(BF16)
    pair_rows = base[0] + dot(pooled, folded[...])
    channels = wlr.shape[1] // 2
    own_left[...] = pair_rows[:, 0:channels].astype(BF16)
    right_land[me] = pair_rows[:, channels:].astype(BF16)

    left_next = send(own_left, left_halo.at[0], left_send.at[0], left_recv.at[0], after)
    left_prev = send(own_left, left_halo.at[1], left_send.at[1], left_recv.at[1], prev)

    @pl.when(has_next)
    def _():
        left_next.start()

    @pl.when(has_prev)
    def _():
        left_prev.start()

    def right_copy(step):
        return send(right_land.at[me], right_land.at[me], right_send.at[step], right_recv.at[me], lax.rem(me + step, n))

    @pl.loop(1, n)
    def _(step):
        right_copy(step).start()

    cols = 512 if width % 512 == 0 else width
    for start in range(0, width, cols):
        stop = start + cols
        track_ref[:, start:stop] = (first[:, start:stop].astype(F32) + dot(attended[...], wo[:, start:stop])).astype(BF16)
    track_out = pltpu.make_async_copy(track_ref, track_hbm, track_sem)
    track_out.start()

    left_ext[...] = jnp.zeros(left_ext.shape, F32)
    left_ext[8:8 + band, :] = own_left[...].astype(F32)

    @pl.when(has_prev)
    def _():
        left_next.wait_recv()
        left_ext[7:8, :] = left_halo[0].astype(F32)[band - 1:band, :]

    @pl.when(has_next)
    def _():
        left_prev.wait_recv()
        left_ext[8 + band:9 + band, :] = left_halo[1].astype(F32)[0:1, :]

    @pl.loop(1, n)
    def _(step):
        slot = lax.rem(me + step, n)
        send(right_land.at[slot], right_land.at[slot], right_send.at[step], right_recv.at[slot], slot).wait_recv()

    @pl.when(has_next)
    def _():
        to_next.wait_send()
        left_next.wait_send()

    @pl.when(has_prev)
    def _():
        to_prev.wait_send()
        left_prev.wait_send()

    for copy in sent:
        copy.wait_send()

    @pl.loop(1, n)
    def _(step):
        right_copy(step).wait_send()

    track_out.wait()


def pair_kernel(
    track_in, left_ext, right_land, wp_hbm, track_out, pair_out,
    track, wp, wide, right_all, act, pair, w_sem, track_sem, pair_sem,
):
    load = pltpu.make_async_copy(wp_hbm, wp, w_sem)
    load.start()
    track_load = pltpu.make_async_copy(track_in, track, track_sem)
    track_load.start()
    columns, channels = right_all.shape
    band = pair.shape[0]
    span = 3 * channels
    right_all[...] = right_land[...].astype(F32).reshape(columns, channels)
    column = lax.broadcasted_iota(jnp.int32, (columns, channels), 0)

    def product(i):
        return (left_ext[i + 7:i + 8, :] * right_all[...]).astype(BF16).astype(F32)

    def activate(i):
        active = jax.nn.gelu(product(i))
        act[i, :, 0:channels] = jnp.where(column == 0, 0.0, pltpu.roll(active, 1, 0)).astype(BF16)
        act[i, :, channels:2 * channels] = active.astype(BF16)
        act[i, :, 2 * channels:] = jnp.where(column == columns - 1, 0.0, pltpu.roll(active, columns - 1, 0)).astype(BF16)

    for i in range(4):
        activate(i)

    load.wait()
    zero = jnp.zeros((span, channels), BF16)
    for r in range(4):
        for o in range(2):
            tap = r - o
            wide[r * span:(r + 1) * span, o * channels:(o + 1) * channels] = (
                wp[tap * span:(tap + 1) * span, :] if 0 <= tap <= 2 else zero
            )
    track_load.wait()
    track_store = pltpu.make_async_copy(track, track_out, track_sem)
    track_store.start()

    def store(i):
        return pltpu.make_async_copy(pair.at[i], pair_out.at[i], pair_sem.at[i])

    for i in range(0, band, 2):
        both = dot(jnp.concatenate([act[i + r] for r in range(4)], axis=1), wide[...])
        for k in (i + 4, i + 5):
            if k < band + 2:
                activate(k)
        for o in range(2):
            pair[i + o] = (product(i + o + 1) + both[:, o * channels:(o + 1) * channels]).astype(BF16)
            store(i + o).start()

    track_store.wait()
    for i in range(band):
        store(i).wait()


def solution(mesh):
    n = mesh.shape["seq"]

    def local(sequence, gain_conv, conv_weight, gain_attn, w_query, w_key, w_value, w_out, w_left, w_right, w_pair):
        rows, width = sequence.shape
        key, val = w_key.shape[1], w_value.shape[1]
        channels = w_left.shape[1]
        band = rows // POOL
        columns = n * band
        chips = n // 2
        value_lanes = (val // 128 + 1) * 128
        tail_rows = rows // PARTS // (128 // (val - 128))
        taps = w_pair.reshape(-1, channels)
        weights = (w_query, w_key, w_value.T, w_out, w_left, w_right)
        anyspace = pl.BlockSpec(memory_space=pl.ANY)
        vmem = pl.BlockSpec(memory_space=pltpu.VMEM)
        dma = pltpu.SemaphoreType.DMA
        steps = max(chips // 2, 1)
        track, left, right = pl.pallas_call(
            functools.partial(kernel, n),
            out_shape=(
                jax.ShapeDtypeStruct((rows, width), BF16),
                jax.ShapeDtypeStruct((band + 16, channels), F32),
                jax.ShapeDtypeStruct((n, band, channels), BF16),
            ),
            in_specs=[vmem] * 2 + [anyspace] * 8,
            out_specs=(anyspace, vmem, vmem),
            scratch_shapes=[pltpu.VMEM((2, width), F32)]
            + [pltpu.VMEM(w.shape, BF16) for w in weights[:4]]
            + [pltpu.VMEM((width, 2 * channels), BF16), pltpu.VMEM((w_out.shape[0], 2 * channels), BF16)]
            + [
                pltpu.VMEM((rows, width), BF16),
                pltpu.VMEM((2, HALO, width), BF16),
                pltpu.VMEM((rows + 2 * HALO, width), F32),
                pltpu.VMEM((rows, width), BF16),
                pltpu.VMEM((rows, width), BF16),
                pltpu.VMEM((HEADS, rows, key), BF16),
                pltpu.VMEM((n, PARTS, key + rows // PARTS + tail_rows, 128), BF16),
                pltpu.VMEM((HEADS, rows, value_lanes), F32),
                pltpu.VMEM((HEADS, rows, 128), F32),
                pltpu.VMEM((rows, HEADS * val), BF16),
                pltpu.VMEM((band, channels), BF16),
                pltpu.VMEM((2, band, channels), BF16),
                pltpu.VMEM((2, key, 4 * (rows // PARTS)), BF16),
                pltpu.VMEM((2, 4 * (rows // PARTS), value_lanes), BF16),
                dma((len(weights) + 2,)),
                dma(()),
                dma((2,)),
                dma((2,)),
                dma((steps + 1, PARTS, SPLIT)),
                dma((steps + 1, PARTS, SPLIT)),
                dma((chips + 1, PARTS, SPLIT)),
                dma((n, PARTS, SPLIT)),
                dma((2,)),
                dma((2,)),
                dma((n,)),
                dma((n,)),
            ],
            compiler_params=pltpu.CompilerParams(
                collective_id=0, has_side_effects=True, vmem_limit_bytes=60 * 1024 * 1024
            ),
        )(sequence, conv_weight, gain_conv, gain_attn, *weights)
        return pl.pallas_call(
            pair_kernel,
            out_shape=(
                jax.ShapeDtypeStruct((rows, width), BF16),
                jax.ShapeDtypeStruct((band, columns, channels), BF16),
            ),
            in_specs=[anyspace, vmem, vmem, anyspace],
            out_specs=(anyspace, anyspace),
            scratch_shapes=[
                pltpu.VMEM((rows, width), BF16),
                pltpu.VMEM(taps.shape, BF16),
                pltpu.VMEM((12 * channels, 2 * channels), BF16),
                pltpu.VMEM((columns, channels), F32),
                pltpu.VMEM((band + 2, columns, 3 * channels), BF16),
                pltpu.VMEM((band, columns, channels), BF16),
                dma(()),
                dma(()),
                dma((band,)),
            ],
            compiler_params=pltpu.CompilerParams(vmem_limit_bytes=60 * 1024 * 1024),
        )(track, left, right, taps)

    placed = (P(("groups", "seq"), None),) + (P(),) * 10
    return jax.shard_map(
        local,
        mesh=mesh,
        in_specs=placed,
        out_specs=(P(("groups", "seq"), None), P(("groups", "seq"), None, None)),
        check_vma=False,
    )
```

```python
import functools
import math

import jax
import jax.numpy as jnp
from jax import lax
from jax.experimental import pallas as pl
from jax.experimental.pallas import tpu as pltpu
from jax.sharding import PartitionSpec as P

HEADS = 8
POOL = 16
HALO = 16
PARTS = 2
SPLIT = 1
F32 = jnp.float32
BF16 = jnp.bfloat16


def dot(a, b):
    return jnp.dot(a, b, preferred_element_type=F32)


def dot_t(a, b):
    return lax.dot_general(a, b, (((1,), (1,)), ((), ())), preferred_element_type=F32)


def rms_norm(values, gain):
    scale = lax.rsqrt(jnp.mean(values * values, axis=-1, keepdims=True) + 1e-06)
    return values * scale * gain


def kernel(
    n,
    seq_ref, conv_ref,
    gconv_hbm, gattn_hbm, wq_hbm, wk_hbm, wv_hbm, wo_hbm, wl_hbm, wr_hbm,
    track_hbm, left_ext, right_land,
    gains, wq, wk, wv, wo, wlr, folded, track_ref,
    halo, padded, first, attn, q_ref, kv, acc, top, attended,
    own_left, left_halo, turned, stage,
    w_sem, track_sem, halo_send, halo_recv, r_send, l_send, p_send, kv_recv,
    left_send, left_recv, right_send, right_recv,
):
    rows, width = seq_ref.shape
    key = wk.shape[1]
    val = wv.shape[0]
    taps = conv_ref.shape[0]
    reach = taps // 2
    part = rows // PARTS
    chips = n // 2
    half = (chips + 1) // 2
    me = lax.axis_index("seq")
    chip = me // 2
    core = me % 2
    partner = chip * 2 + (1 - core)
    pos = jnp.where(chip % 2 == 0, chip // 2, chips - 1 - chip // 2)

    def chip_at(place):
        place = lax.rem(place + 2 * chips, chips)
        return jnp.where(place < half, 2 * place, 2 * (chips - 1 - place) + 1)

    def mine_at(place):
        return chip_at(place) * 2 + core

    def other_at(place):
        return chip_at(place) * 2 + (1 - core)

    barrier = pltpu.get_barrier_semaphore()

    @pl.loop(1, n)
    def _(step):
        pl.semaphore_signal(barrier, inc=1, device_id={"seq": lax.rem(me + step, n)})

    pairs = (
        (wk_hbm, wk), (wv_hbm, wv), (wq_hbm, wq), (wo_hbm, wo),
        (wl_hbm, wlr.at[:, pl.ds(0, wlr.shape[1] // 2)]),
        (wr_hbm, wlr.at[:, pl.ds(wlr.shape[1] // 2, wlr.shape[1] // 2)]),
        (gconv_hbm, gains.at[0]), (gattn_hbm, gains.at[1]),
    )
    loads = [pltpu.make_async_copy(s, d, w_sem.at[i]) for i, (s, d) in enumerate(pairs)]
    for load in loads[6:] + loads[:3] + loads[4:6] + loads[3:4]:
        load.start()

    def send(src, dst, ssem, rsem, to):
        return pltpu.make_async_remote_copy(
            src_ref=src, dst_ref=dst, send_sem=ssem, recv_sem=rsem, device_id={"seq": to}
        )

    has_prev = me > 0
    has_next = me < n - 1
    prev = lax.rem(me + n - 1, n)
    after = lax.rem(me + 1, n)
    to_next = send(seq_ref.at[pl.ds(rows - HALO, HALO)], halo.at[0], halo_send.at[0], halo_recv.at[0], after)
    to_prev = send(seq_ref.at[pl.ds(0, HALO)], halo.at[1], halo_send.at[1], halo_recv.at[1], prev)

    loads[6].wait()
    loads[7].wait()
    gconv = gains[0:1, :]
    strip = 32
    for start in range(0, rows, strip):
        values = seq_ref[start:start + strip, :].astype(F32)
        padded[HALO + start:HALO + start + strip, :] = rms_norm(values, gconv).astype(BF16).astype(F32)

    pl.semaphore_wait(barrier, n - 1)

    @pl.when(has_next)
    def _():
        to_next.start()

    @pl.when(has_prev)
    def _():
        to_prev.start()

    gattn = gains[1:2, :]

    def mix(start):
        total = seq_ref[start:start + strip, :].astype(F32)
        conv = jnp.zeros((strip, width), F32)
        for tap in range(taps):
            base = HALO + start + tap - reach
            conv = conv + conv_ref[tap:tap + 1, :] * padded[base:base + strip, :]
        one = (total + conv).astype(BF16)
        first[start:start + strip, :] = one
        attn[start:start + strip, :] = rms_norm(one.astype(F32), gattn).astype(BF16)

    right_steps = (chips - 1) // 2
    opposite = chips % 2 == 0
    to_right = mine_at(pos + 1)
    to_left = mine_at(pos - 1)
    by_right = PARTS // 2

    size = kv.shape[2] // SPLIT

    def piece(slot, c, u):
        return kv.at[slot, c, pl.ds(u * size, size)]

    def move(slot, c, u, ssem, to):
        return send(piece(slot, c, u), piece(slot, c, u), ssem, kv_recv.at[slot, c, u], to)

    def copy_right(t, c, u):
        return move(mine_at(pos - t), c, u, r_send.at[t, c, u], to_right)

    def copy_left(t, c, u):
        return move(mine_at(pos + t), c, u, l_send.at[t, c, u], to_left)

    def copy_partner(slot, count, c, u):
        return move(slot, c, u, p_send.at[count, c, u], partner)

    def arrived(slot, c, u):
        move(slot, c, u, p_send.at[0, c, u], partner).wait_recv()

    sent = []

    def go(copy):
        copy.start()
        sent.append(copy)

    def pass_right(t, c, u):
        if t < right_steps or (opposite and t == right_steps and c < by_right):
            go(copy_right(t, c, u))

    def pass_left(t, c, u):
        if t < right_steps or (opposite and t == right_steps and c >= by_right):
            go(copy_left(t, c, u))

    tail = val - 128
    fold = part // (128 // tail)

    def project(rows_in, c):
        kv[me, c, 0:key, :] = dot(rows_in, wk[...]).T.astype(BF16)
        values = dot_t(rows_in, wv[...])
        kv[me, c, key:key + part, :] = values[:, 0:128].astype(BF16)
        kv[me, c, key + part:, :] = jnp.concatenate(
            [values[k * fold:(k + 1) * fold, 128:] for k in range(128 // tail)], axis=1
        ).astype(BF16)

    def launch(c):
        for u in range(SPLIT):
            go(copy_partner(me, 0, c, u))
            pass_right(0, c, u)
            pass_left(0, c, u)

    for start in range(strip, rows - strip, strip):
        mix(start)
    loads[0].wait()
    loads[1].wait()
    edge = (rows - part) // 2
    project(attn[edge:rows - edge, :], 0)
    launch(0)

    @pl.when(has_prev)
    def _():
        to_next.wait_recv()
        padded[0:HALO, :] = rms_norm(halo[0].astype(F32), gconv).astype(BF16).astype(F32)

    @pl.when(jnp.logical_not(has_prev))
    def _():
        padded[0:HALO, :] = jnp.zeros((HALO, width), F32)

    @pl.when(has_next)
    def _():
        to_prev.wait_recv()
        padded[HALO + rows:, :] = rms_norm(halo[1].astype(F32), gconv).astype(BF16).astype(F32)

    @pl.when(jnp.logical_not(has_next))
    def _():
        padded[HALO + rows:, :] = jnp.zeros((HALO, width), F32)

    mix(0)
    mix(rows - strip)
    project(jnp.concatenate([attn[0:edge, :], attn[rows - edge:, :]], axis=0), 1)
    launch(1)

    loads[2].wait()
    scale = math.log2(math.e) / math.sqrt(key)
    for h in range(HEADS):
        q_ref[h] = (dot(attn[...], wq[:, h * key:(h + 1) * key]) * scale).astype(BF16)

    lane = lax.broadcasted_iota(jnp.int32, (fold, 128), 1)

    def attend(pieces, initial, b, between):
        for k, (s, c) in enumerate(pieces):
            turned[b, :, k * part:(k + 1) * part] = kv[s, c, 0:key, :]
            stage[b, k * part:(k + 1) * part, 0:128] = kv[s, c, key:key + part, :]
            packed = kv[s, c, key + part:, :].astype(F32)
            for f in range(128 // tail):
                moved = packed if f == 0 else pltpu.roll(packed, 128 - f * tail, 1)
                base = k * part + f * fold
                stage[b, base:base + fold, 128:256] = jnp.where(lane < tail, moved, 1.0).astype(BF16)
        count = len(pieces) * part

        def score(h):
            return dot(q_ref[h], turned[b, :, 0:count])

        def soften(h, scores):
            best = jnp.broadcast_to(jnp.max(scores, axis=1, keepdims=True), (rows, 128))
            old = None
            if not initial:
                old = top[h]
                best = jnp.maximum(old, best)
            return jnp.exp2((scores - jnp.concatenate([best] * (count // 128), axis=1)).astype(BF16)), best, old

        def gather(h, weights, best, old):
            update = dot(weights, stage[b, 0:count, :])
            if initial:
                acc[h] = update
            else:
                factor = jnp.exp2(old - best)
                acc[h] = acc[h] * jnp.concatenate([factor] * (update.shape[1] // 128), axis=1) + update
            top[h] = best

        scores = score(0)
        held = None
        for h in range(HEADS):
            following = score(h + 1) if h + 1 < HEADS else None
            softened = soften(h, scores)
            if held is not None:
                gather(*held)
            held = (h,) + softened
            scores = following
            if h in between:
                between[h]()
        gather(*held)

    for c in range(PARTS):
        for u in range(SPLIT):
            arrived(partner, c, u)
    waiting = ([(s, c) for s in (me, partner) for c in range(PARTS)], [])
    count = 1
    turn = 0

    band = rows // POOL
    member = lax.broadcasted_iota(jnp.int32, (band, rows), 1) // POOL
    pool = jnp.where(member == lax.broadcasted_iota(jnp.int32, (band, rows), 0), 1.0 / POOL, 0.0).astype(BF16)
    base = []
    deep = 256 if wo.shape[0] % 256 == 0 else wo.shape[0]

    def fold_out(turn):
        if turn == 0:
            loads[4].wait()
            loads[5].wait()
            base.append(dot(dot(pool, first[...]).astype(BF16), wlr[...]))
        elif turn == 1:
            loads[3].wait()
        if turn:
            if turn <= wo.shape[0] // deep:
                k = turn - 1
                folded[k * deep:(k + 1) * deep, :] = dot(wo[k * deep:(k + 1) * deep, :], wlr[...]).astype(BF16)

    def work(waiting, turn, between):
        for s, c in waiting[1]:
            for u in range(SPLIT):
                arrived(s, c, u)
        attend(waiting[0] + waiting[1], turn == 0, turn % 2, between)

    def relay(t, c, u, places, count):
        for k, place in enumerate(places):
            slot = mine_at(place)
            arrived(slot, c, u)
            go(copy_partner(slot, count + k, c, u))
            if t < right_steps:
                (pass_right if k == 0 else pass_left)(t + 1, c, u)

    for t in range(right_steps + (1 if opposite else 0)):
        last = t == right_steps
        for c in range(PARTS):
            places = []
            if not last or c < by_right:
                places.append(pos - 1 - t)
            if not last or c >= by_right:
                places.append(pos + 1 + t)
            relay(t, c, 0, places, count)
            work(waiting, turn, {
                u * HEADS // SPLIT - 1: functools.partial(relay, t, c, u, places, count) for u in range(1, SPLIT)
            })
            fold_out(turn)
            turn += 1
            waiting = ([(mine_at(p), c) for p in places], [(other_at(p), c) for p in places])
        count += 2
    for later in range(turn, 1 - (-(wo.shape[0] // deep) // 1)):
        fold_out(later)
    work(waiting, turn, {})

    for pair in range(0, HEADS, 2):
        both = []
        for h in (pair, pair + 1):
            block = acc[h]
            both.append((block[:, :val] * (1.0 / block[:, val:val + 1])).astype(BF16))
        attended[:, pair * val:(pair + 2) * val] = jnp.concatenate(both, axis=1)

    pooled = dot(pool, attended[...]).astype(BF16)
    pair_rows = base[0] + dot(pooled, folded[...])
    channels = wlr.shape[1] // 2
    own_left[...] = pair_rows[:, 0:channels].astype(BF16)
    right_land[me] = pair_rows[:, channels:].astype(BF16)

    left_next = send(own_left, left_halo.at[0], left_send.at[0], left_recv.at[0], after)
    left_prev = send(own_left, left_halo.at[1], left_send.at[1], left_recv.at[1], prev)

    @pl.when(has_next)
    def _():
        left_next.start()

    @pl.when(has_prev)
    def _():
        left_prev.start()

    def right_copy(step):
        return send(right_land.at[me], right_land.at[me], right_send.at[step], right_recv.at[me], lax.rem(me + step, n))

    @pl.loop(1, n)
    def _(step):
        right_copy(step).start()

    cols = 512 if width % 512 == 0 else width
    for start in range(0, width, cols):
        stop = start + cols
        track_ref[:, start:stop] = (first[:, start:stop].astype(F32) + dot(attended[...], wo[:, start:stop])).astype(BF16)
    track_out = pltpu.make_async_copy(track_ref, track_hbm, track_sem)
    track_out.start()

    left_ext[...] = jnp.zeros(left_ext.shape, F32)
    left_ext[8:8 + band, :] = own_left[...].astype(F32)

    @pl.when(has_prev)
    def _():
        left_next.wait_recv()
        left_ext[7:8, :] = left_halo[0].astype(F32)[band - 1:band, :]

    @pl.when(has_next)
    def _():
        left_prev.wait_recv()
        left_ext[8 + band:9 + band, :] = left_halo[1].astype(F32)[0:1, :]

    @pl.loop(1, n)
    def _(step):
        slot = lax.rem(me + step, n)
        send(right_land.at[slot], right_land.at[slot], right_send.at[step], right_recv.at[slot], slot).wait_recv()

    @pl.when(has_next)
    def _():
        to_next.wait_send()
        left_next.wait_send()

    @pl.when(has_prev)
    def _():
        to_prev.wait_send()
        left_prev.wait_send()

    for copy in sent:
        copy.wait_send()

    @pl.loop(1, n)
    def _(step):
        right_copy(step).wait_send()

    track_out.wait()


def pair_kernel(
    track_in, left_ext, right_land, wp_hbm, track_out, pair_out,
    track, wp, wide, right_all, act, pair, w_sem, track_sem, pair_sem,
):
    load = pltpu.make_async_copy(wp_hbm, wp, w_sem)
    load.start()
    track_load = pltpu.make_async_copy(track_in, track, track_sem)
    track_load.start()
    columns, channels = right_all.shape
    band = pair.shape[0]
    span = 3 * channels
    right_all[...] = right_land[...].astype(F32).reshape(columns, channels)
    column = lax.broadcasted_iota(jnp.int32, (columns, channels), 0)

    def product(i):
        return (left_ext[i + 7:i + 8, :] * right_all[...]).astype(BF16).astype(F32)

    def activate(i):
        active = jax.nn.gelu(product(i))
        act[i, :, 0:channels] = jnp.where(column == 0, 0.0, pltpu.roll(active, 1, 0)).astype(BF16)
        act[i, :, channels:2 * channels] = active.astype(BF16)
        act[i, :, 2 * channels:] = jnp.where(column == columns - 1, 0.0, pltpu.roll(active, columns - 1, 0)).astype(BF16)

    for i in range(4):
        activate(i)

    load.wait()
    zero = jnp.zeros((span, channels), BF16)
    for r in range(4):
        for o in range(2):
            tap = r - o
            wide[r * span:(r + 1) * span, o * channels:(o + 1) * channels] = (
                wp[tap * span:(tap + 1) * span, :] if 0 <= tap <= 2 else zero
            )
    track_load.wait()
    track_store = pltpu.make_async_copy(track, track_out, track_sem)
    track_store.start()

    def store(i):
        return pltpu.make_async_copy(pair.at[i], pair_out.at[i], pair_sem.at[i])

    for i in range(0, band, 2):
        both = dot(jnp.concatenate([act[i + r] for r in range(4)], axis=1), wide[...])
        for k in (i + 4, i + 5):
            if k < band + 2:
                activate(k)
        for o in range(2):
            pair[i + o] = (product(i + o + 1) + both[:, o * channels:(o + 1) * channels]).astype(BF16)
            store(i + o).start()

    track_store.wait()
    for i in range(band):
        store(i).wait()


def solution(mesh):
    n = mesh.shape["seq"]

    def local(sequence, gain_conv, conv_weight, gain_attn, w_query, w_key, w_value, w_out, w_left, w_right, w_pair):
        rows, width = sequence.shape
        key, val = w_key.shape[1], w_value.shape[1]
        channels = w_left.shape[1]
        band = rows // POOL
        columns = n * band
        chips = n // 2
        value_lanes = (val // 128 + 1) * 128
        tail_rows = rows // PARTS // (128 // (val - 128))
        taps = w_pair.reshape(-1, channels)
        weights = (w_query, w_key, w_value.T, w_out, w_left, w_right)
        anyspace = pl.BlockSpec(memory_space=pl.ANY)
        vmem = pl.BlockSpec(memory_space=pltpu.VMEM)
        dma = pltpu.SemaphoreType.DMA
        steps = max(chips // 2, 1)
        track, left, right = pl.pallas_call(
            functools.partial(kernel, n),
            out_shape=(
                jax.ShapeDtypeStruct((rows, width), BF16),
                jax.ShapeDtypeStruct((band + 16, channels), F32),
                jax.ShapeDtypeStruct((n, band, channels), BF16),
            ),
            in_specs=[vmem] * 2 + [anyspace] * 8,
            out_specs=(anyspace, vmem, vmem),
            scratch_shapes=[pltpu.VMEM((2, width), F32)]
            + [pltpu.VMEM(w.shape, BF16) for w in weights[:4]]
            + [pltpu.VMEM((width, 2 * channels), BF16), pltpu.VMEM((w_out.shape[0], 2 * channels), BF16)]
            + [
                pltpu.VMEM((rows, width), BF16),
                pltpu.VMEM((2, HALO, width), BF16),
                pltpu.VMEM((rows + 2 * HALO, width), F32),
                pltpu.VMEM((rows, width), BF16),
                pltpu.VMEM((rows, width), BF16),
                pltpu.VMEM((HEADS, rows, key), BF16),
                pltpu.VMEM((n, PARTS, key + rows // PARTS + tail_rows, 128), BF16),
                pltpu.VMEM((HEADS, rows, value_lanes), F32),
                pltpu.VMEM((HEADS, rows, 128), F32),
                pltpu.VMEM((rows, HEADS * val), BF16),
                pltpu.VMEM((band, channels), BF16),
                pltpu.VMEM((2, band, channels), BF16),
                pltpu.VMEM((2, key, 4 * (rows // PARTS)), BF16),
                pltpu.VMEM((2, 4 * (rows // PARTS), value_lanes), BF16),
                dma((len(weights) + 2,)),
                dma(()),
                dma((2,)),
                dma((2,)),
                dma((steps + 1, PARTS, SPLIT)),
                dma((steps + 1, PARTS, SPLIT)),
                dma((chips + 1, PARTS, SPLIT)),
                dma((n, PARTS, SPLIT)),
                dma((2,)),
                dma((2,)),
                dma((n,)),
                dma((n,)),
            ],
            compiler_params=pltpu.CompilerParams(
                collective_id=0, has_side_effects=True, vmem_limit_bytes=60 * 1024 * 1024
            ),
        )(sequence, conv_weight, gain_conv, gain_attn, *weights)
        return pl.pallas_call(
            pair_kernel,
            out_shape=(
                jax.ShapeDtypeStruct((rows, width), BF16),
                jax.ShapeDtypeStruct((band, columns, channels), BF16),
            ),
            in_specs=[anyspace, vmem, vmem, anyspace],
            out_specs=(anyspace, anyspace),
            scratch_shapes=[
                pltpu.VMEM((rows, width), BF16),
                pltpu.VMEM(taps.shape, BF16),
                pltpu.VMEM((12 * channels, 2 * channels), BF16),
                pltpu.VMEM((columns, channels), F32),
                pltpu.VMEM((band + 2, columns, 3 * channels), BF16),
                pltpu.VMEM((band, columns, channels), BF16),
                dma(()),
                dma(()),
                dma((band,)),
            ],
            compiler_params=pltpu.CompilerParams(vmem_limit_bytes=60 * 1024 * 1024),
        )(track, left, right, taps)

    placed = (P(("groups", "seq"), None),) + (P(),) * 10
    return jax.shard_map(
        local,
        mesh=mesh,
        in_specs=placed,
        out_specs=(P(("groups", "seq"), None), P(("groups", "seq"), None, None)),
        check_vma=False,
    )
```
